32 devices in a mesh: grp: 4 (over z), dev: 8 (over y, x, core).
Axes of the slice: x: 2, y: 2, z: 4, core: 2. Of those that a mesh axis runs over, the one named last changes fastest.
Arguments:
- feats: bfloat16 [8192, 1024], P(('grp', 'dev')), may hold values from -6 to 6
- weight: float32 [1024, 1024], replicated, may hold values from -0.1875 to 0.1875
- cotangent: bfloat16 [8192, 1024], P(('grp', 'dev')), may hold values from -6 to 6
- local_adj: int32 [8192, 256], P(('grp', 'dev')), may hold values 0 or 1
- far_mask: int32 [4, 8, 4, 8, 256], P('grp', 'dev'), may hold values 0 or 1
- far_row: int32 [4, 8, 4, 8], P('grp', 'dev'), may hold values from 0 to 255
Outputs:
- activated: bfloat16 [8192, 1024], P(('grp', 'dev'))
- input_grad: float32 [8192, 1024], P(('grp', 'dev'))
- weight_grad: float32 [1024, 1024], P('dev')
The draws below stay inside these ranges and needn't reach their ends.
All inputs are finite; a program needn't handle non-finite values. No bound on the sum of `local_adj` or of `far_mask` on one device may be relied on, other than what follows from the above.
Results may differ from the reference program's by a relative error of at most 0.001.
Values sent between devices are 32-bit elements; how exact they have to be, the bound alone decides.
No kernel may reach another device: no remote copies, remote signals or barrier semaphores. Data moves between devices by JAX's collectives and lax.ppermute only.
A program may use at most 64 MiB of HBM per device.

```python
import jax
import jax.numpy as jnp
from jax import lax

F = 1024
ROWS = 256
CG = 8
NODES = 8192
N_GRP = 4
N_DEV = 8


def set_ends(result, stream_key, least, top_value):
    extent = result.shape
    place = [jax.random.randint(jax.random.fold_in(stream_key, axis), (), 0, extent[axis]) for axis in range(len(extent))]
    result = result.at[tuple(place)].set(least)
    longest = extent.index(max(extent))
    place[longest] = (place[longest] + 1) % extent[longest]
    return result.at[tuple(place)].set(top_value)


def with_spikes(result, key, source, target, blocks, factor):
    def block_of(axis_at):
        return (jnp.arange(result.shape[axis_at]) // (result.shape[axis_at] // blocks)).reshape((-1,) + (1,) * (result.ndim - 1 - axis_at))

    one_side = jax.random.permutation(key, blocks)[block_of(target)]
    second = (block_of(target) + blocks // 2) % blocks
    return jnp.where((block_of(source) == one_side) | (block_of(source) == second), factor * result, result)


def level_of(key, shape, shards, smallest, largest):
    factor_of, own = 1.0, jax.random.fold_in(key, 6)
    for axis_at, parts in shards:
        heights = jnp.exp(jax.random.uniform(jax.random.fold_in(own, axis_at), (parts,), jnp.float32, smallest / len(shards), largest / len(shards)))
        factor_of = factor_of * jnp.repeat(heights, shape[axis_at] // parts).reshape([-1 if axis == axis_at else 1 for axis in range(len(shape))])
    return factor_of


def gaussian(own_key, extent, width, bound, split=(), kind=jnp.bfloat16):
    loudness = level_of(own_key, extent, split, -0.22, 0.18) if split else 1.0
    values = jax.random.normal(own_key, extent, jnp.float32) * width * loudness
    return jnp.minimum(jnp.maximum(values, -bound), bound).astype(kind)


def noise_with(stream_key, dims, scale, reach, shards, heavy, kind=jnp.bfloat16):
    result = scale * jax.random.normal(stream_key, dims, jnp.float32)
    if shards:
        result = result * level_of(stream_key, dims, shards, -0.22, 0.18)
    return jnp.clip(with_spikes(result, jax.random.fold_in(stream_key, 3), *heavy), -reach, reach).astype(kind)


def setup_inputs(seed: int = 0) -> dict:
    splits = jax.random.split(jax.random.key(seed), 7)
    return {
        "feats": noise_with(splits[0], (NODES, F), 1.0, 6.0, ((0, 32),), (0, 1, 32, 2.75)),
        "weight": gaussian(splits[1], (F, F), F ** -0.5, 0.1875, (), jnp.float32),
        "cotangent": gaussian(splits[2], (NODES, F), 1.0, 6.0, ((0, 32),)),
        "local_adj": set_ends((jax.random.randint(splits[3], (NODES, ROWS), 0, 16) < 1).astype(jnp.int32), jax.random.fold_in(splits[3], 1), 0, 1),
        "far_mask": set_ends((jax.random.randint(splits[4], (N_GRP, N_DEV, N_GRP, CG, ROWS), 0, 8) < 1).astype(jnp.int32), jax.random.fold_in(splits[4], 1), 0, 1),
        "far_row": set_ends(jax.random.randint(splits[5], (N_GRP, N_DEV, N_GRP, CG), 0, ROWS), jax.random.fold_in(splits[5], 1), 0, ROWS - 1).astype(jnp.int32),
    }


def send_group(operands):
    group_feats, group_mask = operands
    mask_values = group_mask.astype(jnp.float32)
    outgoing = jnp.einsum("jhcu,juf->jhcf", mask_values, group_feats.astype(jnp.float32), precision=lax.Precision.HIGHEST)
    return outgoing, jnp.sum(mask_values, axis=-1)


def reference(feats, weight, cotangent, local_adj, far_mask, far_row):
    highest = lax.Precision.HIGHEST
    features = feats.reshape(N_GRP, N_DEV, ROWS, F)
    adjacency = local_adj.reshape(N_GRP, N_DEV, ROWS, ROWS)
    cotangents = cotangent.reshape(N_GRP, N_DEV, ROWS, F)
    outgoing, slot_counts = lax.map(send_group, (features, far_mask))
    received = jnp.transpose(outgoing, (2, 1, 0, 3, 4))
    received_counts = jnp.transpose(slot_counts, (2, 1, 0, 3))
    node_index = jnp.arange(ROWS, dtype=jnp.int32)
    slot_total = N_GRP * CG

    def receive_group(operands):
        group_feats, group_adj, arrived, arrived_counts, group_rows, group_cot = operands
        one_hot = (group_rows.reshape(N_DEV, 1, slot_total) == node_index[None, :, None]).astype(jnp.float32)
        adjacency_wide = group_adj.astype(jnp.float32)
        feats_wide = group_feats.astype(jnp.float32)
        local_sum = jnp.einsum("jvu,juf->jvf", adjacency_wide, feats_wide, precision=highest)
        remote_sum = jnp.einsum("jvs,jsf->jvf", one_hot, arrived.reshape(N_DEV, slot_total, F), precision=highest)
        degree = jnp.sum(adjacency_wide, axis=-1) + jnp.einsum("jvs,js->jv", one_hot, arrived_counts.reshape(N_DEV, slot_total), precision=highest)
        inverse = 1.0 / (1.0 + degree)
        aggregate = (feats_wide + local_sum + remote_sum) * inverse[..., None]
        preact = jnp.einsum("jvf,fk->jvk", aggregate, weight, precision=highest)
        sigmoid_pre = jax.nn.sigmoid(preact)
        activated = (preact * sigmoid_pre).astype(jnp.bfloat16)
        pre_grad = group_cot.astype(jnp.float32) * sigmoid_pre * (1.0 + preact * (1.0 - sigmoid_pre))
        scaled_grad = pre_grad * inverse[..., None]
        back_local = scaled_grad + jnp.einsum("jvu,jvf->juf", adjacency_wide, scaled_grad, precision=highest)
        slot_rows = jnp.einsum("jvs,jvf->jsf", one_hot, scaled_grad, precision=highest).reshape(N_DEV, N_GRP, CG, F)
        weight_part = jnp.einsum("jvf,jvk->fk", aggregate, pre_grad, precision=highest)
        return activated, back_local, slot_rows, weight_part

    activated, back_local, slot_rows, weight_parts = lax.map(
        receive_group, (features, adjacency, received, received_counts, far_row, cotangents))
    returned = jnp.transpose(slot_rows, (2, 1, 0, 3, 4))

    def finish_group(operands):
        group_back, group_returned, group_mask = operands
        remote_back = jnp.einsum("jhcu,jhcf->juf", group_mask.astype(jnp.float32), group_returned, precision=highest)
        total_back = group_back + remote_back
        return jnp.einsum("juf,kf->juk", total_back, weight, precision=highest)

    input_grad = lax.map(finish_group, (back_local, returned, far_mask))
    weight_grad = jnp.sum(weight_parts, axis=0)
    total_nodes = N_GRP * N_DEV * ROWS
    return activated.reshape(total_nodes, F), input_grad.reshape(total_nodes, F), weight_grad
```

```python
import functools

import jax
import jax.numpy as jnp
from jax import lax
from jax.experimental import pallas as pl
from jax.experimental.pallas import tpu as pltpu
from jax.sharding import PartitionSpec as P


AXES = ("grp", "dev")
LANES = 128
EIGHTHS = (4, 4)
CHUNKS = len(EIGHTHS)
LIMIT = 16 << 20
F32 = jnp.float32
BF16 = jnp.bfloat16
VMEM = pl.BlockSpec(memory_space=pltpu.VMEM)
SMEM = pl.BlockSpec(memory_space=pltpu.SMEM)
HBM = pl.BlockSpec(memory_space=pltpu.HBM)


def in_hbm(value):
    return pltpu.with_memory_space_constraint(value, pltpu.HBM)


def split(value):
    high = value.astype(BF16)
    return high, (value - high.astype(F32)).astype(BF16)


def dot(left, right, dims=((1,), (0,))):
    return lax.dot_general(left, right, (dims, ((), ())), preferred_element_type=F32)


def dot_three(left, right, dims=((1,), (0,))):
    left_high, left_low = left
    right_high, right_low = right
    return dot(left_high, right_high, dims) + (
        dot(left_high, right_low, dims) + dot(left_low, right_high, dims)
    )


def call(kernel, out_shape, in_specs, flops, bytes_moved, scratch=(), outs=None, aliases=None):
    many = isinstance(out_shape, (tuple, list))
    return pl.pallas_call(
        kernel,
        out_shape=out_shape,
        in_specs=in_specs,
        out_specs=outs or ([VMEM] * len(out_shape) if many else VMEM),
        input_output_aliases=aliases or {},
        scratch_shapes=list(scratch),
        compiler_params=pltpu.CompilerParams(vmem_limit_bytes=LIMIT),
        cost_estimate=pl.CostEstimate(
            flops=flops, bytes_accessed=bytes_moved, transcendentals=0
        ),
    )


def border_kernel(groups, width, me_ref, feats_hbm, mask_hbm, *refs):
    out_refs, (feats_ref, mask_ref, sems) = refs[:groups], refs[groups:]
    copies = [
        pltpu.make_async_copy(source, target, sems.at[k])
        for k, (source, target) in enumerate(
            ((feats_hbm, feats_ref), (mask_hbm, mask_ref))
        )
    ]
    for copy in copies:
        copy.start()
    for copy in copies:
        copy.wait()
    feats = feats_ref[...]
    lanes = feats.shape[1]
    for step, out_ref in enumerate(out_refs):
        target = lax.rem(me_ref[0] + step, groups)
        flags = mask_ref[pl.ds(pl.multiple_of(target * width, width), width), :]
        flags = flags.astype(F32)
        out_ref[:, :lanes] = dot(flags.astype(BF16), feats)
        counts = jnp.sum(flags, axis=1, keepdims=True)
        out_ref[:, lanes:] = jnp.broadcast_to(counts, (width, LANES))


def local_kernel(
    pieces, feats_hbm, adj_hbm, weight_hbm, base_ref, degree_ref, high_ref, low_ref,
    feats_ref, adj_ref, weight_ref, sems,
):
    step = weight_hbm.shape[0] // pieces
    copies = [
        pltpu.make_async_copy(feats_hbm, feats_ref, sems.at[0]),
        pltpu.make_async_copy(adj_hbm, adj_ref, sems.at[1]),
    ]
    for k in range(pieces):
        rows = pl.ds(k * step, step)
        copies.append(
            pltpu.make_async_copy(
                weight_hbm.at[rows, :], weight_ref.at[rows, :], sems.at[2 + k]
            )
        )
    for copy in copies:
        copy.start()
    copies[0].wait()
    copies[1].wait()
    feats = feats_ref[...]
    flags = adj_ref[...].astype(F32)
    base_ref[...] = feats.astype(F32) + dot(flags.astype(BF16), feats)
    degree = jnp.sum(flags, axis=1, keepdims=True)
    degree_ref[...] = jnp.broadcast_to(degree, degree_ref.shape)
    for k in range(pieces):
        copies[2 + k].wait()
        rows = pl.ds(k * step, step)
        high, low = split(weight_ref[rows, :])
        high_ref[rows, :] = high
        low_ref[rows, :] = low


def aggregate_kernel(groups, parts, orders, grp_ref, dev_ref, rows_ref, base_ref, degree_ref, *refs):
    arrived = jnp.concatenate([ref[...] for ref in refs[:groups]], axis=0)
    agg_ref, inverse_ref, hot_ref = refs[groups : groups + 3]
    flipped, turned_ref, flags_ref = refs[groups + 3 : -2], refs[-2], refs[-1]
    nodes, lanes = base_ref.shape
    width = rows_ref.shape[1]
    index = lax.broadcasted_iota(jnp.int32, (1, nodes), 1)
    for step in range(groups):
        source = lax.rem(grp_ref[0] + (groups - step), groups)
        for slot in range(width):
            at = step * width + slot
            flags_ref[at : at + 1, :] = jnp.where(index == rows_ref[source, slot], 1.0, 0.0)
    one_hot = flags_ref[...].astype(BF16)
    hot_ref[...] = one_hot
    high, low = split(arrived)
    first = ((0,), (0,))
    remote = dot(one_hot, high, first) + dot(one_hot, low, first)
    inverse = 1.0 / (1.0 + degree_ref[...] + remote[:, lanes:])
    inverse_ref[...] = inverse
    agg = (base_ref[...] + remote[:, :lanes]) * inverse[:, :1]
    agg_ref[...] = agg
    turned_ref[...] = agg.T
    for which, ref in enumerate(flipped):
        for place, block in enumerate(orders(dev_ref[0], which)):
            picked = turned_ref[pl.ds(pl.multiple_of(block * parts, parts), parts), :]
            ref[place * parts : (place + 1) * parts, :] = picked


def forward_kernel(start, agg_ref, high_ref, low_ref, cot_ref, act_ref, grad_ref):
    at = slice(start, start + act_ref.shape[1])
    preact = dot_three(split(agg_ref[...]), (high_ref[:, at], low_ref[:, at]))
    sigmoid = 1.0 / (1.0 + jnp.exp(-preact))
    act_ref[...] = (preact * sigmoid).astype(BF16)
    slope = sigmoid * (1.0 + preact * (1.0 - sigmoid))
    grad_ref[...] = cot_ref[:, at].astype(F32) * slope


def term_kernel(count, *refs):
    total = None
    for agg_ref, grad_ref in zip(refs[:count], refs[count : 2 * count]):
        part = dot_three(split(agg_ref[...]), split(grad_ref[...]))
        total = part if total is None else total + part
    outs = refs[2 * count :]
    start = 0
    for ref in outs:
        ref[...] = total[start : start + ref.shape[0]]
        start += ref.shape[0]


def slots_kernel(width, hot_ref, inverse_ref, *refs):
    grads, acts = refs[:CHUNKS], refs[CHUNKS : 2 * CHUNKS]
    outs, act_ref = refs[2 * CHUNKS : -1], refs[-1]
    one_hot = hot_ref[...]
    start = 0
    for ref, act in zip(grads, acts):
        stop = start + ref.shape[1]
        act_ref[:, start:stop] = act[...]
        high, low = split(ref[...] * inverse_ref[:, :1])
        rows = dot(one_hot, high) + dot(one_hot, low)
        for step, out in enumerate(outs):
            out[:, start:stop] = rows[step * width : (step + 1) * width]
        start = stop


def last_kernel(start, count, total_ref, *refs):
    came, (out_ref, sum_ref, sem) = refs[:count], refs[-3:]
    total = total_ref[...]
    for ref in came:
        total = total + ref[...]
    sum_ref[...] = total
    columns = pl.ds(start, total.shape[1])
    copy = pltpu.make_async_copy(sum_ref, out_ref.at[:, columns], sem)
    copy.start()
    copy.wait()


def backward_kernel(
    groups, width, me_ref, adj_ref, mask_ref, inverse_ref, high_ref, low_ref, *refs
):
    grads, refs = refs[:CHUNKS], refs[CHUNKS:]
    arrived, out_ref = refs[:groups], refs[groups]
    flags = adj_ref[...].astype(F32).T.astype(BF16)
    pieces = [
        mask_ref[pl.ds(pl.multiple_of(lax.rem(me_ref[0] + s, groups) * width, width), width), :]
        for s in range(groups)
    ]
    border = jnp.concatenate(pieces, axis=0).astype(F32).T.astype(BF16)
    total, start = None, 0
    for ref in grads:
        stop = start + ref.shape[1]
        scaled = ref[...] * inverse_ref[:, :1]
        high, low = split(scaled)
        back = scaled + dot(flags, high) + dot(flags, low)
        high, low = split(jnp.concatenate([r[:, start:stop] for r in arrived], axis=0))
        back = back + dot(border, high) + dot(border, low)
        part = dot_three(split(back), (high_ref[:, start:stop], low_ref[:, start:stop]), ((1,), (1,)))
        total = part if total is None else total + part
        start = stop
    out_ref[...] = total


def factors(number):
    found, prime = [], 2
    while number > 1:
        while number % prime == 0:
            found.append(prime)
            number //= prime
        prime += 1
    return found


def stages_of(number):
    stages, stride = [], 1
    for factor in factors(number):
        stages.append((stride, factor))
        stride *= factor
    return stages


def turned(stages, shift):
    run = 0
    while run < len(stages) and stages[run][1] == stages[0][1]:
        run += 1
    shift = shift % run if run else 0
    return stages[shift:run] + stages[:shift] + stages[run:]


def shifted(index, stage, amount):
    stride, factor = stage
    if isinstance(index, int):
        digit = index // stride % factor
        return index + ((digit + amount) % factor - digit) * stride
    digit = lax.rem(lax.div(index, stride), factor)
    return index + (lax.rem(digit + amount, factor) - digit) * stride


def pick(condition_index, values):
    result = values[0]
    for place, value in enumerate(values[1:], 1):
        result = jnp.where(condition_index == place, value, result)
    return result


def body(groups, devs, feats, weight, cotangent, local_adj, far_mask, far_row):
    nodes, lanes = feats.shape
    width = far_mask.shape[3]
    slots = groups * width
    outer = weight.shape[1]
    share = weight.shape[0] // devs
    edges = [outer * sum(EIGHTHS[:c]) // sum(EIGHTHS) for c in range(CHUNKS + 1)]
    me_grp, me_dev = lax.axis_index("grp"), lax.axis_index("dev")
    me = me_grp.reshape(1).astype(jnp.int32)
    dev = me_dev.reshape(1).astype(jnp.int32)
    mask = far_mask.reshape(slots, nodes)
    shape = jax.ShapeDtypeStruct

    def permute(value, pairs):
        return lax.ppermute(value, AXES, pairs)

    def over_grp(step):
        return [
            (g * devs + d, ((g + step) % groups) * devs + d)
            for g in range(groups)
            for d in range(devs)
        ]

    def over(moves):
        return [
            (g * devs + d, moves(g, d)[0] * devs + moves(g, d)[1])
            for g in range(groups)
            for d in range(devs)
        ]

    stages = stages_of(devs)
    first, rest = stages[0], stages[1:]
    pair = first[1]
    kinds = [turned(rest, k) for k in range(pair)]
    grp_kinds = [turned(stages_of(groups), k) for k in range(pair)]
    inner = devs // pair

    def orders(dev, which):
        dev = shifted(dev, first, which)
        lists = []
        for kind in kinds:
            found = [dev]
            for stage in reversed(kind):
                found = [shifted(d, stage, e) for e in range(stage[1]) for d in found]
            lists.append(found)
        return [pick(lax.rem(dev, pair), same) for same in zip(*lists)]

    outgoing = call(
        functools.partial(border_kernel, groups, width),
        [shape((width, lanes + LANES), F32)] * groups,
        [SMEM, HBM, HBM],
        2 * slots * nodes * lanes,
        feats.size * 2 + mask.size * 4,
        [
            pltpu.VMEM(feats.shape, BF16),
            pltpu.VMEM(mask.shape, jnp.int32),
            pltpu.SemaphoreType.DMA((2,)),
        ],
    )(me, in_hbm(feats), in_hbm(mask))
    received = [outgoing[0]] + [
        permute(outgoing[k], over_grp(k)) for k in range(1, groups)
    ]
    pieces = 4
    base, degree, high, low = call(
        functools.partial(local_kernel, pieces),
        [shape((nodes, lanes), F32), shape((nodes, LANES), F32)]
        + [shape(weight.shape, BF16)] * 2,
        [HBM, HBM, HBM],
        2 * nodes * nodes * lanes,
        nodes * lanes * 6 + weight.size * 8,
        [
            pltpu.VMEM(feats.shape, BF16),
            pltpu.VMEM(local_adj.shape, jnp.int32),
            pltpu.VMEM(weight.shape, F32),
            pltpu.SemaphoreType.DMA((2 + pieces,)),
        ],
    )(in_hbm(feats), in_hbm(local_adj), in_hbm(weight))
    agg, inverse, hot, *flipped = call(
        functools.partial(aggregate_kernel, groups, share, orders),
        [
            shape((nodes, lanes), F32),
            shape((nodes, LANES), F32),
            shape((slots, nodes), BF16),
        ]
        + [shape((inner * share, nodes), F32)] * pair,
        [SMEM, SMEM, SMEM] + [VMEM] * (2 + groups),
        4 * slots * nodes * lanes,
        nodes * lanes * 16,
        [pltpu.VMEM((lanes, nodes), F32), pltpu.VMEM((slots, nodes), F32)],
    )(me, dev, far_row.reshape(groups, width), base, degree, *received)

    def to_partner(value, k):
        return permute(value, over(lambda g, d: (g, shifted(d, first, k))))

    aggs = [flipped[0]] + [to_partner(flipped[k], k) for k in range(1, pair)]

    acts, grads = [], []
    sends, keeps = [], []
    half = rest[0][1] if rest else 1
    block = inner * share // half
    for c in range(CHUNKS):
        piece = edges[c + 1] - edges[c]
        act, grad = call(
            functools.partial(forward_kernel, edges[c]),
            [shape((nodes, piece), BF16), shape((nodes, piece), F32)],
            [VMEM] * 4,
            6 * nodes * lanes * piece,
            lanes * piece * 4 + nodes * lanes * 4,
        )(agg, high, low, cotangent)
        acts.append(act)
        grads.append(grad)
    for c in range(CHUNKS):
        piece = edges[c + 1] - edges[c]
        chunk = [grads[c]] + [to_partner(grads[c], k) for k in range(1, pair)]
        outs = call(
            functools.partial(term_kernel, pair),
            [shape((block, piece), F32)] * half,
            [VMEM] * (2 * pair),
            6 * nodes * pair * inner * share * piece,
            inner * share * piece * 4 + nodes * pair * (piece + inner * share) * 4,
        )(*aggs, *chunk)
        keeps.append(outs[0])
        sends.append(outs[1:])

    totals = []
    for c in range(CHUNKS):
        keep, send = keeps[c], sends[c]
        for level in range(len(rest)):
            size = [kind[level][1] for kind in kinds][0]
            came = [
                permute(
                    send[k - 1], over(lambda g, d, k=k: (g, shifted(d, kinds[d % pair][level], k)))
                )
                for k in range(1, size)
            ]
            if level + 1 < len(rest):
                split_in = kinds[0][level + 1][1]
                step = keep.shape[0] // split_in
                parts = []
                for k in range(split_in):
                    at = slice(k * step, (k + 1) * step)
                    parts.append(functools.reduce(jnp.add, [keep[at]] + [v[at] for v in came]))
                keep, send = parts[0], parts[1:]
            else:
                keep = functools.reduce(jnp.add, [keep] + came)
        totals.append(keep)
    pick_slots = call(
        functools.partial(slots_kernel, width),
        [shape((width, outer), F32)] * groups + [shape((nodes, outer), BF16)],
        [VMEM] * (2 + 2 * CHUNKS),
        4 * slots * nodes * outer,
        nodes * outer * 4,
    )
    *slot_rows, activated = pick_slots(hot, inverse, *grads, *acts)
    weight_grad = None
    levels = len(grp_kinds[0])
    for level in range(levels):
        size = grp_kinds[0][level][1]
        for c in range(CHUNKS):
            came = [
                permute(
                    totals[c],
                    over(lambda g, d, k=k: (shifted(g, grp_kinds[d % pair][level], k), d)),
                )
                for k in range(1, size)
            ]
            if level + 1 < levels:
                totals[c] = functools.reduce(jnp.add, [totals[c]] + came)
                continue
            piece = edges[c + 1] - edges[c]
            before = [] if weight_grad is None else [weight_grad]
            weight_grad = call(
                functools.partial(last_kernel, edges[c], len(came)),
                shape((share, outer), F32),
                [VMEM] * (1 + len(came)) + [HBM] * len(before),
                share * piece,
                share * piece * 4,
                [pltpu.VMEM((share, piece), F32), pltpu.SemaphoreType.DMA],
                HBM,
                {1 + len(came): 0} if before else None,
            )(totals[c], *came, *before)
    returned = [slot_rows[0]] + [
        permute(slot_rows[k], over_grp(groups - k)) for k in range(1, groups)
    ]
    back = call(
        functools.partial(backward_kernel, groups, width),
        shape((nodes, lanes), F32),
        [SMEM] + [VMEM] * (5 + CHUNKS + groups),
        6 * nodes * lanes * outer,
        nodes * outer * 8 + weight.size * 4,
    )
    input_grad = back(me, local_adj, mask, inverse, high, low, *grads, *returned)
    return activated, input_grad, weight_grad


def solution(mesh):
    in_specs = (
        P(AXES, None),
        P(),
        P(AXES, None),
        P(AXES, None),
        P("grp", "dev", None, None, None),
        P("grp", "dev", None, None),
    )
    out_specs = (P(AXES, None), P(AXES, None), P("dev", None))
    groups, devs = mesh.shape["grp"], mesh.shape["dev"]

    def run(*args):
        return body(groups, devs, *args)

    return jax.shard_map(
        run, mesh=mesh, in_specs=in_specs, out_specs=out_specs, check_vma=False
    )
```

```python
import functools

import jax
import jax.numpy as jnp
from jax import lax
from jax.experimental import pallas as pl
from jax.experimental.pallas import tpu as pltpu
from jax.sharding import PartitionSpec as P


AXES = ("grp", "dev")
LANES = 128
EIGHTHS = (4, 4)
CHUNKS = len(EIGHTHS)
SHIFTS = ((1, 2), (2, 0))
LIMIT = 16 << 20
F32 = jnp.float32
BF16 = jnp.bfloat16
VMEM = pl.BlockSpec(memory_space=pltpu.VMEM)
SMEM = pl.BlockSpec(memory_space=pltpu.SMEM)
HBM = pl.BlockSpec(memory_space=pltpu.HBM)


def in_hbm(value):
    return pltpu.with_memory_space_constraint(value, pltpu.HBM)


def split(value):
    high = value.astype(BF16)
    return high, (value - high.astype(F32)).astype(BF16)


def dot(left, right, dims=((1,), (0,))):
    return lax.dot_general(left, right, (dims, ((), ())), preferred_element_type=F32)


def dot_three(left, right, dims=((1,), (0,))):
    left_high, left_low = left
    right_high, right_low = right
    return dot(left_high, right_high, dims) + (
        dot(left_high, right_low, dims) + dot(left_low, right_high, dims)
    )


def call(kernel, out_shape, in_specs, flops, bytes_moved, scratch=(), outs=None, aliases=None):
    many = isinstance(out_shape, (tuple, list))
    return pl.pallas_call(
        kernel,
        out_shape=out_shape,
        in_specs=in_specs,
        out_specs=outs or ([VMEM] * len(out_shape) if many else VMEM),
        input_output_aliases=aliases or {},
        scratch_shapes=list(scratch),
        compiler_params=pltpu.CompilerParams(vmem_limit_bytes=LIMIT),
        cost_estimate=pl.CostEstimate(
            flops=flops, bytes_accessed=bytes_moved, transcendentals=0
        ),
    )


def border_kernel(groups, width, me_ref, feats_hbm, mask_hbm, *refs):
    out_refs, (feats_ref, mask_ref, sems) = refs[:groups], refs[groups:]
    copies = [
        pltpu.make_async_copy(source, target, sems.at[k])
        for k, (source, target) in enumerate(
            ((feats_hbm, feats_ref), (mask_hbm, mask_ref))
        )
    ]
    for copy in copies:
        copy.start()
    for copy in copies:
        copy.wait()
    feats = feats_ref[...]
    lanes = feats.shape[1]
    for step, out_ref in enumerate(out_refs):
        target = lax.rem(me_ref[0] + step, groups)
        flags = mask_ref[pl.ds(pl.multiple_of(target * width, width), width), :]
        flags = flags.astype(F32)
        out_ref[:, :lanes] = dot(flags.astype(BF16), feats)
        counts = jnp.sum(flags, axis=1, keepdims=True)
        out_ref[:, lanes:] = jnp.broadcast_to(counts, (width, LANES))


def local_kernel(
    pieces, feats_hbm, adj_hbm, weight_hbm, base_ref, degree_ref, high_ref, low_ref,
    feats_ref, adj_ref, weight_ref, sems,
):
    step = weight_hbm.shape[0] // pieces
    copies = [
        pltpu.make_async_copy(feats_hbm, feats_ref, sems.at[0]),
        pltpu.make_async_copy(adj_hbm, adj_ref, sems.at[1]),
    ]
    for k in range(pieces):
        rows = pl.ds(k * step, step)
        copies.append(
            pltpu.make_async_copy(
                weight_hbm.at[rows, :], weight_ref.at[rows, :], sems.at[2 + k]
            )
        )
    for copy in copies:
        copy.start()
    copies[0].wait()
    copies[1].wait()
    feats = feats_ref[...]
    flags = adj_ref[...].astype(F32)
    base_ref[...] = feats.astype(F32) + dot(flags.astype(BF16), feats)
    degree = jnp.sum(flags, axis=1, keepdims=True)
    degree_ref[...] = jnp.broadcast_to(degree, degree_ref.shape)
    for k in range(pieces):
        copies[2 + k].wait()
        rows = pl.ds(k * step, step)
        high, low = split(weight_ref[rows, :])
        high_ref[rows, :] = high
        low_ref[rows, :] = low


def aggregate_kernel(groups, parts, orders, grp_ref, dev_ref, rows_ref, base_ref, degree_ref, *refs):
    arrived = jnp.concatenate([ref[...] for ref in refs[:groups]], axis=0)
    agg_ref, inverse_ref, hot_ref = refs[groups : groups + 3]
    flipped, turned_ref, flags_ref = refs[groups + 3 : -2], refs[-2], refs[-1]
    nodes, lanes = base_ref.shape
    width = rows_ref.shape[1]
    index = lax.broadcasted_iota(jnp.int32, (1, nodes), 1)
    for step in range(groups):
        source = lax.rem(grp_ref[0] + (groups - step), groups)
        for slot in range(width):
            at = step * width + slot
            flags_ref[at : at + 1, :] = jnp.where(index == rows_ref[source, slot], 1.0, 0.0)
    one_hot = flags_ref[...].astype(BF16)
    hot_ref[...] = one_hot
    high, low = split(arrived)
    first = ((0,), (0,))
    remote = dot(one_hot, high, first) + dot(one_hot, low, first)
    inverse = 1.0 / (1.0 + degree_ref[...] + remote[:, lanes:])
    inverse_ref[...] = inverse
    agg = (base_ref[...] + remote[:, :lanes]) * inverse[:, :1]
    agg_ref[...] = agg
    turned_ref[...] = agg.T
    for which, ref in enumerate(flipped):
        for place, block in enumerate(orders(dev_ref[0], which)):
            picked = turned_ref[pl.ds(pl.multiple_of(block * parts, parts), parts), :]
            ref[place * parts : (place + 1) * parts, :] = picked


def forward_kernel(start, agg_ref, high_ref, low_ref, cot_ref, act_ref, grad_ref):
    at = slice(start, start + act_ref.shape[1])
    preact = dot_three(split(agg_ref[...]), (high_ref[:, at], low_ref[:, at]))
    sigmoid = 1.0 / (1.0 + jnp.exp(-preact))
    act_ref[...] = (preact * sigmoid).astype(BF16)
    slope = sigmoid * (1.0 + preact * (1.0 - sigmoid))
    grad_ref[...] = cot_ref[:, at].astype(F32) * slope


def term_kernel(count, rows, places, grp_ref, dev_ref, *refs):
    total = None
    for agg_ref, grad_ref in zip(refs[:count], refs[count : 2 * count]):
        part = dot_three(split(agg_ref[...]), split(grad_ref[...]))
        total = part if total is None else total + part
    outs, total_ref = refs[2 * count : -1], refs[-1]
    total_ref[...] = total
    each = outs[0].shape[0] // rows
    for place, block in enumerate(places(grp_ref[0], dev_ref[0])):
        ref, at = outs[place // each], place % each * rows
        ref[at : at + rows, :] = total_ref[pl.ds(pl.multiple_of(block * rows, rows), rows), :]


def slots_kernel(width, hot_ref, inverse_ref, *refs):
    grads, acts = refs[:CHUNKS], refs[CHUNKS : 2 * CHUNKS]
    outs, act_ref = refs[2 * CHUNKS : -1], refs[-1]
    one_hot = hot_ref[...]
    start = 0
    for ref, act in zip(grads, acts):
        stop = start + ref.shape[1]
        act_ref[:, start:stop] = act[...]
        high, low = split(ref[...] * inverse_ref[:, :1])
        rows = dot(one_hot, high) + dot(one_hot, low)
        for step, out in enumerate(outs):
            out[:, start:stop] = rows[step * width : (step + 1) * width]
        start = stop


def last_kernel(start, stage, grp_ref, *refs):
    pieces, (out_ref, sum_ref, sem) = refs[: stage[1]], refs[-3:]
    rows = pieces[0].shape[0]
    for step, ref in enumerate(pieces):
        digit = lax.rem(lax.div(grp_ref[0], stage[0]) + stage[1] - step, stage[1])
        sum_ref[pl.ds(pl.multiple_of(digit * rows, rows), rows), :] = ref[...]
    columns = pl.ds(start, sum_ref.shape[1])
    copy = pltpu.make_async_copy(sum_ref, out_ref.at[:, columns], sem)
    copy.start()
    copy.wait()


def backward_kernel(
    groups, width, me_ref, adj_ref, mask_ref, inverse_ref, high_ref, low_ref, *refs
):
    grads, refs = refs[:CHUNKS], refs[CHUNKS:]
    arrived, out_ref = refs[:groups], refs[groups]
    flags = adj_ref[...].astype(F32).T.astype(BF16)
    pieces = [
        mask_ref[pl.ds(pl.multiple_of(lax.rem(me_ref[0] + s, groups) * width, width), width), :]
        for s in range(groups)
    ]
    border = jnp.concatenate(pieces, axis=0).astype(F32).T.astype(BF16)
    total, start = None, 0
    for ref in grads:
        stop = start + ref.shape[1]
        scaled = ref[...] * inverse_ref[:, :1]
        high, low = split(scaled)
        back = scaled + dot(flags, high) + dot(flags, low)
        high, low = split(jnp.concatenate([r[:, start:stop] for r in arrived], axis=0))
        back = back + dot(border, high) + dot(border, low)
        part = dot_three(split(back), (high_ref[:, start:stop], low_ref[:, start:stop]), ((1,), (1,)))
        total = part if total is None else total + part
        start = stop
    out_ref[...] = total


def factors(number):
    found, prime = [], 2
    while number > 1:
        while number % prime == 0:
            found.append(prime)
            number //= prime
        prime += 1
    return found


def stages_of(number):
    stages, stride = [], 1
    for factor in factors(number):
        stages.append((stride, factor))
        stride *= factor
    return stages


def shifted(index, stage, amount):
    stride, factor = stage
    if isinstance(index, int):
        digit = index // stride % factor
        return index + ((digit + amount) % factor - digit) * stride
    digit = lax.rem(lax.div(index, stride), factor)
    return index + (lax.rem(digit + amount, factor) - digit) * stride


def plan(groups, devs):
    dev_stages, grp_stages = stages_of(devs), stages_of(groups)
    scatter = [("grp", grp_stages[0])]
    scatter += [("dev", stage) for stage in reversed(dev_stages[1:])]
    return dev_stages[0], scatter, grp_stages[1:]


def turned(stages, shift):
    run = 0
    while run < len(stages) and stages[run][1][1] == stages[0][1][1]:
        run += 1
    shift %= run
    return stages[shift:run] + stages[:shift] + stages[run:]


def moved(grp, dev, stage, amount):
    axis, steps = stage
    if axis == "grp":
        return shifted(grp, steps, amount), dev
    return grp, shifted(dev, steps, amount)


def pick(condition_index, values):
    result = values[0]
    for place, value in enumerate(values[1:], 1):
        result = jnp.where(condition_index == place, value, result)
    return result


def body(groups, devs, feats, weight, cotangent, local_adj, far_mask, far_row):
    nodes, lanes = feats.shape
    width = far_mask.shape[3]
    slots = groups * width
    outer = weight.shape[1]
    share = weight.shape[0] // devs
    edges = [outer * sum(EIGHTHS[:c]) // sum(EIGHTHS) for c in range(CHUNKS + 1)]
    me_grp, me_dev = lax.axis_index("grp"), lax.axis_index("dev")
    me = me_grp.reshape(1).astype(jnp.int32)
    dev = me_dev.reshape(1).astype(jnp.int32)
    mask = far_mask.reshape(slots, nodes)
    shape = jax.ShapeDtypeStruct

    def permute(value, pairs):
        return lax.ppermute(value, AXES, pairs)

    def over_grp(step):
        return [
            (g * devs + d, ((g + step) % groups) * devs + d)
            for g in range(groups)
            for d in range(devs)
        ]

    def over(moves):
        return [
            (g * devs + d, moves(g, d)[0] * devs + moves(g, d)[1])
            for g in range(groups)
            for d in range(devs)
        ]

    first, scatter, exchange = plan(groups, devs)
    pair = first[1]
    inner = devs // pair
    parts = scatter[0][1][1]
    rows = share // parts

    def kinds(c):
        return [turned(scatter, SHIFTS[c][digit % 2]) for digit in range(pair)]

    def orders(dev, which):
        digit = lax.rem(lax.rem(dev, pair) + which, pair)
        return [place * pair + digit for place in range(inner)]

    def places(c, grp, dev):
        lists = []
        for kind in kinds(c):
            found = [(grp, dev)]
            for stage in reversed(kind):
                found = [moved(*at, stage, e) for e in range(stage[1][1]) for at in found]
            lists.append(
                [
                    lax.div(d, pair) * parts
                    + lax.rem(lax.div(g, scatter[0][1][0]), parts)
                    for g, d in found
                ]
            )
        return [pick(lax.rem(dev, pair), same) for same in zip(*lists)]

    outgoing = call(
        functools.partial(border_kernel, groups, width),
        [shape((width, lanes + LANES), F32)] * groups,
        [SMEM, HBM, HBM],
        2 * slots * nodes * lanes,
        feats.size * 2 + mask.size * 4,
        [
            pltpu.VMEM(feats.shape, BF16),
            pltpu.VMEM(mask.shape, jnp.int32),
            pltpu.SemaphoreType.DMA((2,)),
        ],
    )(me, in_hbm(feats), in_hbm(mask))
    received = [outgoing[0]] + [
        permute(outgoing[k], over_grp(k)) for k in range(1, groups)
    ]
    pieces = 4
    base, degree, high, low = call(
        functools.partial(local_kernel, pieces),
        [shape((nodes, lanes), F32), shape((nodes, LANES), F32)]
        + [shape(weight.shape, BF16)] * 2,
        [HBM, HBM, HBM],
        2 * nodes * nodes * lanes,
        nodes * lanes * 6 + weight.size * 8,
        [
            pltpu.VMEM(feats.shape, BF16),
            pltpu.VMEM(local_adj.shape, jnp.int32),
            pltpu.VMEM(weight.shape, F32),
            pltpu.SemaphoreType.DMA((2 + pieces,)),
        ],
    )(in_hbm(feats), in_hbm(local_adj), in_hbm(weight))
    agg, inverse, hot, *flipped = call(
        functools.partial(aggregate_kernel, groups, share, orders),
        [
            shape((nodes, lanes), F32),
            shape((nodes, LANES), F32),
            shape((slots, nodes), BF16),
        ]
        + [shape((inner * share, nodes), F32)] * pair,
        [SMEM, SMEM, SMEM] + [VMEM] * (2 + groups),
        4 * slots * nodes * lanes,
        nodes * lanes * 16,
        [pltpu.VMEM((lanes, nodes), F32), pltpu.VMEM((slots, nodes), F32)],
    )(me, dev, far_row.reshape(groups, width), base, degree, *received)

    def to_partner(value, k):
        return permute(value, over(lambda g, d: (g, shifted(d, first, k))))

    aggs = [flipped[0]] + [to_partner(flipped[k], k) for k in range(1, pair)]

    acts, grads = [], []
    sends, keeps = [], []
    half = scatter[0][1][1]
    block = inner * share // half
    for c in range(CHUNKS):
        piece = edges[c + 1] - edges[c]
        act, grad = call(
            functools.partial(forward_kernel, edges[c]),
            [shape((nodes, piece), BF16), shape((nodes, piece), F32)],
            [VMEM] * 4,
            6 * nodes * lanes * piece,
            lanes * piece * 4 + nodes * lanes * 4,
        )(agg, high, low, cotangent)
        acts.append(act)
        grads.append(grad)
    for c in range(CHUNKS):
        piece = edges[c + 1] - edges[c]
        chunk = [grads[c]] + [to_partner(grads[c], k) for k in range(1, pair)]
        outs = call(
            functools.partial(term_kernel, pair, rows, functools.partial(places, c)),
            [shape((block, piece), F32)] * half,
            [SMEM, SMEM] + [VMEM] * (2 * pair),
            6 * nodes * pair * inner * share * piece,
            inner * share * piece * 4 + nodes * pair * (piece + inner * share) * 4,
            [pltpu.VMEM((inner * share, piece), F32)],
        )(me, dev, *aggs, *chunk)
        keeps.append(outs[0])
        sends.append(outs[1:])

    totals = []
    for c in range(CHUNKS):
        keep, send = keeps[c], sends[c]
        order = kinds(c)
        for level in range(len(scatter)):
            came = [
                permute(
                    send[k - 1],
                    over(lambda g, d, k=k: moved(g, d, order[d % pair][level], k)),
                )
                for k in range(1, order[0][level][1][1])
            ]
            if level + 1 == len(scatter):
                keep = functools.reduce(jnp.add, [keep] + came)
                continue
            split_in = order[0][level + 1][1][1]
            step = keep.shape[0] // split_in
            halves = []
            for k in range(split_in):
                at = slice(k * step, (k + 1) * step)
                halves.append(functools.reduce(jnp.add, [keep[at]] + [v[at] for v in came]))
            keep, send = halves[0], halves[1:]
        for stage in exchange:
            came = [
                permute(keep, over(lambda g, d, k=k: (shifted(g, stage, k), d)))
                for k in range(1, stage[1])
            ]
            keep = functools.reduce(jnp.add, [keep] + came)
        totals.append(keep)

    pick_slots = call(
        functools.partial(slots_kernel, width),
        [shape((width, outer), F32)] * groups + [shape((nodes, outer), BF16)],
        [VMEM] * (2 + 2 * CHUNKS),
        4 * slots * nodes * outer,
        nodes * outer * 4,
    )
    *slot_rows, activated = pick_slots(hot, inverse, *grads, *acts)
    weight_grad = None
    for c in range(CHUNKS):
        stage = scatter[0][1]
        came = [
            permute(totals[c], over(lambda g, d, k=k: (shifted(g, stage, k), d)))
            for k in range(1, stage[1])
        ]
        piece = edges[c + 1] - edges[c]
        before = [] if weight_grad is None else [weight_grad]
        weight_grad = call(
            functools.partial(last_kernel, edges[c], stage),
            shape((share, outer), F32),
            [SMEM] + [VMEM] * stage[1] + [HBM] * len(before),
            share * piece,
            share * piece * 4,
            [pltpu.VMEM((share, piece), F32), pltpu.SemaphoreType.DMA],
            HBM,
            {1 + stage[1]: 0} if before else None,
        )(me, totals[c], *came, *before)
    returned = [slot_rows[0]] + [
        permute(slot_rows[k], over_grp(groups - k)) for k in range(1, groups)
    ]
    back = call(
        functools.partial(backward_kernel, groups, width),
        shape((nodes, lanes), F32),
        [SMEM] + [VMEM] * (5 + CHUNKS + groups),
        6 * nodes * lanes * outer,
        nodes * outer * 8 + weight.size * 4,
    )
    input_grad = back(me, local_adj, mask, inverse, high, low, *grads, *returned)
    return activated, input_grad, weight_grad


def solution(mesh):
    in_specs = (
        P(AXES, None),
        P(),
        P(AXES, None),
        P(AXES, None),
        P("grp", "dev", None, None, None),
        P("grp", "dev", None, None),
    )
    out_specs = (P(AXES, None), P(AXES, None), P("dev", None))
    groups, devs = mesh.shape["grp"], mesh.shape["dev"]

    def run(*args):
        return body(groups, devs, *args)

    return jax.shard_map(
        run, mesh=mesh, in_specs=in_specs, out_specs=out_specs, check_vma=False
    )
```

```python
import functools

import jax
import jax.numpy as jnp
from jax import lax
from jax.experimental import pallas as pl
from jax.experimental.pallas import tpu as pltpu
from jax.sharding import PartitionSpec as P


AXES = ("grp", "dev")
LANES = 128
EIGHTHS = (4, 4)
CHUNKS = len(EIGHTHS)
SHIFTS = ((1, 2), (2, 0))
LIMIT = 16 << 20
F32 = jnp.float32
BF16 = jnp.bfloat16
VMEM = pl.BlockSpec(memory_space=pltpu.VMEM)
SMEM = pl.BlockSpec(memory_space=pltpu.SMEM)
HBM = pl.BlockSpec(memory_space=pltpu.HBM)


def in_hbm(value):
    return pltpu.with_memory_space_constraint(value, pltpu.HBM)


def split(value):
    high = value.astype(BF16)
    return high, (value - high.astype(F32)).astype(BF16)


def dot(left, right, dims=((1,), (0,))):
    return lax.dot_general(left, right, (dims, ((), ())), preferred_element_type=F32)


def dot_three(left, right, dims=((1,), (0,))):
    left_high, left_low = left
    right_high, right_low = right
    return dot(left_high, right_high, dims) + (
        dot(left_high, right_low, dims) + dot(left_low, right_high, dims)
    )


def call(kernel, out_shape, in_specs, flops, bytes_moved, scratch=(), outs=None, aliases=None):
    many = isinstance(out_shape, (tuple, list))
    return pl.pallas_call(
        kernel,
        out_shape=out_shape,
        in_specs=in_specs,
        out_specs=outs or ([VMEM] * len(out_shape) if many else VMEM),
        input_output_aliases=aliases or {},
        scratch_shapes=list(scratch),
        compiler_params=pltpu.CompilerParams(vmem_limit_bytes=LIMIT),
        cost_estimate=pl.CostEstimate(
            flops=flops, bytes_accessed=bytes_moved, transcendentals=0
        ),
    )


def border_kernel(groups, width, me_ref, feats_hbm, mask_hbm, *refs):
    out_refs, (feats_ref, mask_ref, sems) = refs[:groups], refs[groups:]
    copies = [
        pltpu.make_async_copy(source, target, sems.at[k])
        for k, (source, target) in enumerate(
            ((feats_hbm, feats_ref), (mask_hbm, mask_ref))
        )
    ]
    for copy in copies:
        copy.start()
    for copy in copies:
        copy.wait()
    feats = feats_ref[...]
    lanes = feats.shape[1]
    for step, out_ref in enumerate(out_refs):
        target = lax.rem(me_ref[0] + step, groups)
        flags = mask_ref[pl.ds(pl.multiple_of(target * width, width), width), :]
        flags = flags.astype(F32)
        out_ref[:, :lanes] = dot(flags.astype(BF16), feats)
        counts = jnp.sum(flags, axis=1, keepdims=True)
        out_ref[:, lanes:] = jnp.broadcast_to(counts, (width, LANES))


def local_kernel(
    pieces, feats_hbm, adj_hbm, weight_hbm, base_ref, degree_ref, high_ref, low_ref,
    feats_ref, adj_ref, weight_ref, sems,
):
    step = weight_hbm.shape[0] // pieces
    copies = [
        pltpu.make_async_copy(feats_hbm, feats_ref, sems.at[0]),
        pltpu.make_async_copy(adj_hbm, adj_ref, sems.at[1]),
    ]
    for k in range(pieces):
        rows = pl.ds(k * step, step)
        copies.append(
            pltpu.make_async_copy(
                weight_hbm.at[rows, :], weight_ref.at[rows, :], sems.at[2 + k]
            )
        )
    for copy in copies:
        copy.start()
    copies[0].wait()
    copies[1].wait()
    feats = feats_ref[...]
    flags = adj_ref[...].astype(F32)
    base_ref[...] = feats.astype(F32) + dot(flags.astype(BF16), feats)
    degree = jnp.sum(flags, axis=1, keepdims=True)
    degree_ref[...] = jnp.broadcast_to(degree, degree_ref.shape)
    for k in range(pieces):
        copies[2 + k].wait()
        rows = pl.ds(k * step, step)
        high, low = split(weight_ref[rows, :])
        high_ref[rows, :] = high
        low_ref[rows, :] = low


def aggregate_kernel(
    groups, parts, orders, grp_ref, dev_ref, rows_ref, base_ref, degree_ref, *refs
):
    arrived, refs = refs[:groups], refs[groups:]
    agg_high_ref, agg_low_ref, inverse_ref, hot_ref = refs[:4]
    flipped, (turned_ref, arrived_ref, flags_ref) = refs[4:-3], refs[-3:]
    nodes, lanes = base_ref.shape
    width = arrived[0].shape[0]
    for step, ref in enumerate(arrived):
        source = lax.rem(grp_ref[0] + (groups - step), groups)
        arrived_ref[pl.ds(pl.multiple_of(source * width, width), width), :] = ref[...]
    index = lax.broadcasted_iota(jnp.int32, (nodes, width), 0)
    for group in range(groups):
        flags = jnp.where(rows_ref[group : group + 1, :] == index, 1.0, 0.0)
        flags_ref[:, group * width : (group + 1) * width] = flags
    one_hot = flags_ref[...].astype(BF16)
    hot_ref[...] = one_hot
    high, low = split(arrived_ref[...])
    remote = dot(one_hot, high) + dot(one_hot, low)
    inverse = 1.0 / (1.0 + degree_ref[...] + remote[:, lanes:])
    inverse_ref[...] = inverse
    agg = (base_ref[...] + remote[:, :lanes]) * inverse[:, :1]
    agg_high_ref[...], agg_low_ref[...] = split(agg)
    turned_ref[...] = agg.T
    for which, ref in enumerate(flipped):
        for place, block in enumerate(orders(dev_ref[0], which)):
            picked = turned_ref[pl.ds(pl.multiple_of(block * parts, parts), parts), :]
            ref[place * parts : (place + 1) * parts, :] = picked


def forward_kernel(start, agg_high_ref, agg_low_ref, high_ref, low_ref, cot_ref, act_ref, grad_ref):
    at = slice(start, start + act_ref.shape[1])
    preact = dot_three((agg_high_ref[...], agg_low_ref[...]), (high_ref[:, at], low_ref[:, at]))
    sigmoid = 1.0 / (1.0 + jnp.exp(-preact))
    act_ref[...] = (preact * sigmoid).astype(BF16)
    slope = sigmoid * (1.0 + preact * (1.0 - sigmoid))
    grad_ref[...] = cot_ref[:, at].astype(F32) * slope


def term_kernel(count, rows, places, grp_ref, dev_ref, *refs):
    total = None
    for agg_ref, grad_ref in zip(refs[:count], refs[count : 2 * count]):
        part = dot_three(split(agg_ref[...]), split(grad_ref[...]))
        total = part if total is None else total + part
    outs, total_ref = refs[2 * count : -1], refs[-1]
    total_ref[...] = total
    each = outs[0].shape[0] // rows
    for place, block in enumerate(places(grp_ref[0], dev_ref[0])):
        ref, at = outs[place // each], place % each * rows
        ref[at : at + rows, :] = total_ref[pl.ds(pl.multiple_of(block * rows, rows), rows), :]


def slots_kernel(width, groups, grp_ref, hot_ref, inverse_ref, *refs):
    grads, acts = refs[:CHUNKS], refs[CHUNKS : 2 * CHUNKS]
    outs, act_ref, rows_ref = refs[2 * CHUNKS : -2], refs[-2], refs[-1]
    one_hot = hot_ref[...]
    start = 0
    for ref, act in zip(grads, acts):
        stop = start + ref.shape[1]
        act_ref[:, start:stop] = act[...]
        high, low = split(ref[...] * inverse_ref[:, :1])
        first = ((0,), (0,))
        rows_ref[:, start:stop] = dot(one_hot, high, first) + dot(one_hot, low, first)
        start = stop
    for step, out in enumerate(outs):
        source = lax.rem(grp_ref[0] + (groups - step), groups)
        out[...] = rows_ref[pl.ds(pl.multiple_of(source * width, width), width), :]


def last_kernel(start, stage, grp_ref, *refs):
    pieces, (out_ref, sum_ref, sem) = refs[: stage[1]], refs[-3:]
    rows = pieces[0].shape[0]
    for step, ref in enumerate(pieces):
        digit = lax.rem(lax.div(grp_ref[0], stage[0]) + stage[1] - step, stage[1])
        sum_ref[pl.ds(pl.multiple_of(digit * rows, rows), rows), :] = ref[...]
    columns = pl.ds(start, sum_ref.shape[1])
    copy = pltpu.make_async_copy(sum_ref, out_ref.at[:, columns], sem)
    copy.start()
    copy.wait()


def backward_kernel(
    groups, width, me_ref, adj_ref, mask_ref, inverse_ref, high_ref, low_ref, *refs
):
    grads, refs = refs[:CHUNKS], refs[CHUNKS:]
    arrived, out_ref = refs[:groups], refs[groups]
    flags = adj_ref[...].astype(F32).T.astype(BF16)
    pieces = [
        mask_ref[pl.ds(pl.multiple_of(lax.rem(me_ref[0] + s, groups) * width, width), width), :]
        for s in range(groups)
    ]
    border = jnp.concatenate(pieces, axis=0).astype(F32).T.astype(BF16)
    total, start = None, 0
    for ref in grads:
        stop = start + ref.shape[1]
        scaled = ref[...] * inverse_ref[:, :1]
        high, low = split(scaled)
        back = scaled + dot(flags, high) + dot(flags, low)
        high, low = split(jnp.concatenate([r[:, start:stop] for r in arrived], axis=0))
        back = back + dot(border, high) + dot(border, low)
        part = dot_three(split(back), (high_ref[:, start:stop], low_ref[:, start:stop]), ((1,), (1,)))
        total = part if total is None else total + part
        start = stop
    out_ref[...] = total


def factors(number):
    found, prime = [], 2
    while number > 1:
        while number % prime == 0:
            found.append(prime)
            number //= prime
        prime += 1
    return found


def stages_of(number):
    stages, stride = [], 1
    for factor in factors(number):
        stages.append((stride, factor))
        stride *= factor
    return stages


def shifted(index, stage, amount):
    stride, factor = stage
    if isinstance(index, int):
        digit = index // stride % factor
        return index + ((digit + amount) % factor - digit) * stride
    digit = lax.rem(lax.div(index, stride), factor)
    return index + (lax.rem(digit + amount, factor) - digit) * stride


def plan(groups, devs):
    dev_stages, grp_stages = stages_of(devs), stages_of(groups)
    scatter = [("grp", grp_stages[0])]
    scatter += [("dev", stage) for stage in reversed(dev_stages[1:])]
    return dev_stages[0], scatter, grp_stages[1:]


def turned(stages, shift):
    run = 0
    while run < len(stages) and stages[run][1][1] == stages[0][1][1]:
        run += 1
    flip, shift = divmod(shift, 3)
    shift %= run
    front = stages[shift:run] + stages[:shift]
    if flip:
        front = front[:1] + front[:0:-1]
    return front + stages[run:]


def moved(grp, dev, stage, amount):
    axis, steps = stage
    if axis == "grp":
        return shifted(grp, steps, amount), dev
    return grp, shifted(dev, steps, amount)


def pick(condition_index, values):
    result = values[0]
    for place, value in enumerate(values[1:], 1):
        result = jnp.where(condition_index == place, value, result)
    return result


def body(groups, devs, feats, weight, cotangent, local_adj, far_mask, far_row):
    nodes, lanes = feats.shape
    width = far_mask.shape[3]
    slots = groups * width
    outer = weight.shape[1]
    share = weight.shape[0] // devs
    edges = [outer * sum(EIGHTHS[:c]) // sum(EIGHTHS) for c in range(CHUNKS + 1)]
    me_grp, me_dev = lax.axis_index("grp"), lax.axis_index("dev")
    me = me_grp.reshape(1).astype(jnp.int32)
    dev = me_dev.reshape(1).astype(jnp.int32)
    mask = far_mask.reshape(slots, nodes)
    shape = jax.ShapeDtypeStruct

    def permute(value, pairs):
        return lax.ppermute(value, AXES, pairs)

    def over_grp(step):
        return [
            (g * devs + d, ((g + step) % groups) * devs + d)
            for g in range(groups)
            for d in range(devs)
        ]

    def over(moves):
        return [
            (g * devs + d, moves(g, d)[0] * devs + moves(g, d)[1])
            for g in range(groups)
            for d in range(devs)
        ]

    first, scatter, exchange = plan(groups, devs)
    pair = first[1]
    inner = devs // pair
    parts = scatter[0][1][1]
    rows = share // parts

    def kinds(c):
        return [turned(scatter, SHIFTS[c][digit % 2]) for digit in range(pair)]

    def orders(dev, which):
        digit = lax.rem(lax.rem(dev, pair) + which, pair)
        return [place * pair + digit for place in range(inner)]

    def places(c, grp, dev):
        lists = []
        for kind in kinds(c):
            found = [(grp, dev)]
            for stage in reversed(kind):
                found = [moved(*at, stage, e) for e in range(stage[1][1]) for at in found]
            lists.append(
                [
                    lax.div(d, pair) * parts
                    + lax.rem(lax.div(g, scatter[0][1][0]), parts)
                    for g, d in found
                ]
            )
        return [pick(lax.rem(dev, pair), same) for same in zip(*lists)]

    outgoing = call(
        functools.partial(border_kernel, groups, width),
        [shape((width, lanes + LANES), F32)] * groups,
        [SMEM, HBM, HBM],
        2 * slots * nodes * lanes,
        feats.size * 2 + mask.size * 4,
        [
            pltpu.VMEM(feats.shape, BF16),
            pltpu.VMEM(mask.shape, jnp.int32),
            pltpu.SemaphoreType.DMA((2,)),
        ],
    )(me, in_hbm(feats), in_hbm(mask))
    received = [outgoing[0]] + [
        permute(outgoing[k], over_grp(k)) for k in range(1, groups)
    ]
    pieces = 4
    base, degree, high, low = call(
        functools.partial(local_kernel, pieces),
        [shape((nodes, lanes), F32), shape((nodes, LANES), F32)]
        + [shape(weight.shape, BF16)] * 2,
        [HBM, HBM, HBM],
        2 * nodes * nodes * lanes,
        nodes * lanes * 6 + weight.size * 8,
        [
            pltpu.VMEM(feats.shape, BF16),
            pltpu.VMEM(local_adj.shape, jnp.int32),
            pltpu.VMEM(weight.shape, F32),
            pltpu.SemaphoreType.DMA((2 + pieces,)),
        ],
    )(in_hbm(feats), in_hbm(local_adj), in_hbm(weight))
    agg_high, agg_low, inverse, hot, *flipped = call(
        functools.partial(aggregate_kernel, groups, share, orders),
        [shape((nodes, lanes), BF16)] * 2
        + [shape((nodes, LANES), F32), shape((nodes, slots), BF16)]
        + [shape((inner * share, nodes), F32)] * pair,
        [SMEM, SMEM] + [VMEM] * (3 + groups),
        4 * slots * nodes * lanes,
        nodes * lanes * 16,
        [
            pltpu.VMEM((lanes, nodes), F32),
            pltpu.VMEM((slots, lanes + LANES), F32),
            pltpu.VMEM((nodes, slots), F32),
        ],
    )(me, dev, far_row.reshape(groups, width), base, degree, *received)

    def to_partner(value, k):
        return permute(value, over(lambda g, d: (g, shifted(d, first, k))))

    aggs = [flipped[0]] + [to_partner(flipped[k], k) for k in range(1, pair)]

    acts, grads = [], []
    sends, keeps = [], []
    half = scatter[0][1][1]
    block = inner * share // half
    for c in range(CHUNKS):
        piece = edges[c + 1] - edges[c]
        act, grad = call(
            functools.partial(forward_kernel, edges[c]),
            [shape((nodes, piece), BF16), shape((nodes, piece), F32)],
            [VMEM] * 5,
            6 * nodes * lanes * piece,
            lanes * piece * 4 + nodes * lanes * 4,
        )(agg_high, agg_low, high, low, cotangent)
        acts.append(act)
        grads.append(grad)
    for c in range(CHUNKS):
        piece = edges[c + 1] - edges[c]
        chunk = [grads[c]] + [to_partner(grads[c], k) for k in range(1, pair)]
        outs = call(
            functools.partial(term_kernel, pair, rows, functools.partial(places, c)),
            [shape((block, piece), F32)] * half,
            [SMEM, SMEM] + [VMEM] * (2 * pair),
            6 * nodes * pair * inner * share * piece,
            inner * share * piece * 4 + nodes * pair * (piece + inner * share) * 4,
            [pltpu.VMEM((inner * share, piece), F32)],
        )(me, dev, *aggs, *chunk)
        keeps.append(outs[0])
        sends.append(outs[1:])

    totals = []
    for c in range(CHUNKS):
        keep, send = keeps[c], sends[c]
        order = kinds(c)
        for level in range(len(scatter)):
            came = [
                permute(
                    send[k - 1],
                    over(lambda g, d, k=k: moved(g, d, order[d % pair][level], k)),
                )
                for k in range(1, order[0][level][1][1])
            ]
            if level + 1 == len(scatter):
                keep = functools.reduce(jnp.add, [keep] + came)
                continue
            split_in = order[0][level + 1][1][1]
            step = keep.shape[0] // split_in
            halves = []
            for k in range(split_in):
                at = slice(k * step, (k + 1) * step)
                halves.append(functools.reduce(jnp.add, [keep[at]] + [v[at] for v in came]))
            keep, send = halves[0], halves[1:]
        for stage in exchange:
            came = [
                permute(keep, over(lambda g, d, k=k: (shifted(g, stage, k), d)))
                for k in range(1, stage[1])
            ]
            keep = functools.reduce(jnp.add, [keep] + came)
        totals.append(keep)

    pick_slots = call(
        functools.partial(slots_kernel, width, groups),
        [shape((width, outer), F32)] * groups + [shape((nodes, outer), BF16)],
        [SMEM] + [VMEM] * (2 + 2 * CHUNKS),
        4 * slots * nodes * outer,
        nodes * outer * 4,
        [pltpu.VMEM((slots, outer), F32)],
    )
    *slot_rows, activated = pick_slots(me, hot, inverse, *grads, *acts)
    weight_grad = None
    for c in range(CHUNKS):
        stage = scatter[0][1]
        came = [
            permute(totals[c], over(lambda g, d, k=k: (shifted(g, stage, k), d)))
            for k in range(1, stage[1])
        ]
        piece = edges[c + 1] - edges[c]
        before = [] if weight_grad is None else [weight_grad]
        weight_grad = call(
            functools.partial(last_kernel, edges[c], stage),
            shape((share, outer), F32),
            [SMEM] + [VMEM] * stage[1] + [HBM] * len(before),
            share * piece,
            share * piece * 4,
            [pltpu.VMEM((share, piece), F32), pltpu.SemaphoreType.DMA],
            HBM,
            {1 + stage[1]: 0} if before else None,
        )(me, totals[c], *came, *before)
    returned = [slot_rows[0]] + [
        permute(slot_rows[k], over_grp(groups - k)) for k in range(1, groups)
    ]
    back = call(
        functools.partial(backward_kernel, groups, width),
        shape((nodes, lanes), F32),
        [SMEM] + [VMEM] * (5 + CHUNKS + groups),
        6 * nodes * lanes * outer,
        nodes * outer * 8 + weight.size * 4,
    )
    input_grad = back(me, local_adj, mask, inverse, high, low, *grads, *returned)
    return activated, input_grad, weight_grad


def solution(mesh):
    in_specs = (
        P(AXES, None),
        P(),
        P(AXES, None),
        P(AXES, None),
        P("grp", "dev", None, None, None),
        P("grp", "dev", None, None),
    )
    out_specs = (P(AXES, None), P(AXES, None), P("dev", None))
    groups, devs = mesh.shape["grp"], mesh.shape["dev"]

    def run(*args):
        return body(groups, devs, *args)

    return jax.shard_map(
        run, mesh=mesh, in_specs=in_specs, out_specs=out_specs, check_vma=False
    )
```
